32 devices in a mesh: dp: 2 (over x), row: 4 (over z), col: 4 (over y, core).
Axes of the slice: x: 2, y: 2, z: 4, core: 2. Of those that a mesh axis runs over, the one named last changes fastest.
Arguments:
- hidden: bfloat16 [8192, 896], P(('dp', 'row'), 'col'), may hold values from -6 to 6
- segments: int32 [2, 4, 4, 256], P('dp', 'col', 'row'), may hold values from 0 to 3, never falling along the last dimension, each value on 1 to 128 neighbouring positions
- attn_gain: bfloat16 [2, 896], P(None, 'col'), may hold values from 0.5 to 1.5
- qkv_weight: bfloat16 [2, 896, 1152], P(None, 'col', 'row'), as said below
- qkv_bias: bfloat16 [2, 1152], P(None, 'row'), may hold values from -3 to 3
- out_weight: bfloat16 [2, 896, 896], P(None, 'row', 'col'), may hold values from -0.09375 to 0.09375
- mlp_gain: bfloat16 [2, 896], P(None, 'col'), may hold values from 0.5 to 1.5
- gate_up_weight: bfloat16 [2, 896, 2, 4864], P(None, 'col', None, 'row'), may hold values from -0.1875 to 0.1875
- down_weight: bfloat16 [2, 4864, 896], P(None, 'row', 'col'), may hold values from -0.15625 to 0.15625
- cotangent: bfloat16 [8192, 896], P(('dp', 'row'), 'col'), may hold values from -6 to 6
Outputs:
- result: bfloat16 [8192, 896], P(('dp', 'row'), 'col')
- grad_hidden: float32 [8192, 896], P(('dp', 'row'), 'col')
- attn_gain_grad: float32 [2, 896], P(None, 'col')
- qkv_weight_grad: float32 [2, 896, 1152], P(None, 'col', 'row')
- qkv_bias_grad: float32 [2, 1152], P(None, 'row')
- out_weight_grad: float32 [2, 896, 896], P(None, 'row', 'col')
- mlp_gain_grad: float32 [2, 896], P(None, 'col')
- gate_up_grad: float32 [2, 896, 2, 4864], P(None, 'col', None, 'row')
- down_grad: float32 [2, 4864, 896], P(None, 'row', 'col')
The draws below stay inside these ranges and needn't reach their ends.
Inputs may be any that keep to these rules, and one draw needn't show every extreme that they name: `segments`: along each packed sequence of 256 tokens the numbers never fall; each number covers at most 128 tokens, and some covers exactly that many. `qkv_weight`: entries lie within 48 * 896 ** -0.5 in magnitude.
All inputs are finite; a program needn't handle non-finite values.
Results may differ from the reference program's by a relative error of at most 0.023.
Values may be sent and summed in bfloat16 or wider, within the bound.
A program may use at most 256 MiB of HBM per device.

```python
import math
import jax
import jax.numpy as jnp
import numpy as np
from jax import lax

D = 896
HEADS = 14
KV = 2
HEAD = 64
FF = 4864
SEQ_LEN = 256
LAYERS = 2
QKV = 1152
TOKENS = 8192
N_DP = 2
N_ROW = 4
N_COL = 4


def draw_qkv_weight(key, part):
    base = jax.random.truncated_normal(key, -6.0, 6.0, (LAYERS, D, QKV), jnp.float32)
    column = jnp.arange(QKV, dtype=jnp.int32)
    factor = jnp.where(column >= QKV - KV * HEAD, 8.0, 1.0).astype(jnp.float32)
    return (base * factor[None, None, :] * D ** (-0.5)).astype(jnp.bfloat16)


def steps_of(own_key, shape, split, low, top_value):
    factor_of = 1.0
    for axis_at, blocks in split:
        heights = jax.random.uniform(jax.random.fold_in(jax.random.fold_in(own_key, 6), axis_at), (blocks,), jnp.float32, low / len(split), top_value / len(split))
        factor_of = factor_of * jnp.repeat(jnp.exp(heights), shape[axis_at] // blocks).reshape((-1,) + (1,) * (len(shape) - 1 - axis_at))
    return factor_of


def length_profile(amount, total, bound, slope):
    loads = [(1 << 20) // math.isqrt(rank ** slope) + 1 for rank in range(2, amount + 1)]
    spare, given = total - bound - (amount - 1), [1] * (amount - 1)
    while spare > 0:
        movable = [i for i in range(amount - 1) if given[i] < bound]
        mass, remaining = sum([loads[i] for i in movable]), spare
        for i in movable:
            more = min(bound - given[i], max(1, remaining * loads[i] // mass), spare)
            given[i] = given[i] + more
            spare = spare - more
    return np.array([bound] + given)


def ragged_sizes(own_key, count, total, bound, slope):
    if count == 2:
        one = jax.random.randint(own_key, (), max(1, total - bound), min(bound, total - 1) + 1)
        return jnp.stack([one, total - one])
    sizes = jnp.asarray(length_profile(count, total, bound, slope), jnp.int32)
    pairs = (count - 1) // 2
    donor, sink = sizes[1:1 + 2 * pairs:2], sizes[2:2 + 2 * pairs:2]
    room = jnp.minimum(donor - 1, bound - sink)
    shifted = jax.random.randint(jax.random.fold_in(own_key, 1), (pairs,), 0, 1 << 20) % (room + 1)
    sizes = sizes.at[1:1 + 2 * pairs:2].set(donor - shifted).at[2:2 + 2 * pairs:2].set(sink + shifted)
    return sizes[jax.random.permutation(jax.random.fold_in(own_key, 2), count)]


def gaussian(rng, shape, scale, reach, pieces=(), held_as=jnp.bfloat16):
    array = scale * jax.random.normal(rng, shape, jnp.float32)
    if pieces:
        array = array * steps_of(rng, shape, pieces, -0.22, 0.18)
    return jnp.clip(array, -reach, reach).astype(held_as)


def setup_inputs(seed: int = 0) -> dict:
    key_list = jax.random.split(jax.random.key(seed), 11)
    hidden = gaussian(key_list[0], (TOKENS, D), 1.0, 6.0, ((0, 8), (1, 4)))
    segments = jax.vmap(lambda own: jnp.searchsorted(jnp.cumsum(ragged_sizes(own, 4, SEQ_LEN, SEQ_LEN // 2, 0)), jnp.arange(SEQ_LEN), side="right"))(jax.random.split(key_list[1], N_DP * N_COL * N_ROW)).reshape((N_DP, N_COL, N_ROW, SEQ_LEN)).astype(jnp.int32)
    attn_gain = jnp.clip(1.0 + 0.1 * jax.random.normal(key_list[2], (LAYERS, D), jnp.float32), 0.5, 1.5).astype(jnp.bfloat16)
    qkv_weight = draw_qkv_weight(jax.random.fold_in(key_list[10], 71), 0)
    qkv_bias = gaussian(key_list[4], (LAYERS, QKV), 0.5, 3.0, ((1, 4),))
    out_weight = gaussian(key_list[5], (LAYERS, D, D), (4 * D) ** -0.5, 0.09375, ((1, 4), (2, 4)))
    mlp_gain = jnp.clip(1.0 + 0.1 * jax.random.normal(key_list[6], (LAYERS, D), jnp.float32), 0.5, 1.5).astype(jnp.bfloat16)
    gate_up_weight = gaussian(key_list[7], (LAYERS, D, 2, FF), D ** -0.5, 0.1875, ((1, 4), (3, 4)))
    down_weight = gaussian(key_list[8], (LAYERS, FF, D), (FF // 4) ** -0.5, 0.15625, ((1, 4), (2, 4)))
    cotangent = gaussian(key_list[9], (TOKENS, D), 1.0, 6.0, ((0, 8), (1, 4)))
    return {"hidden": hidden, "segments": segments, "attn_gain": attn_gain, "qkv_weight": qkv_weight, "qkv_bias": qkv_bias, "out_weight": out_weight, "mlp_gain": mlp_gain, "gate_up_weight": gate_up_weight, "down_weight": down_weight, "cotangent": cotangent}


@jax.custom_vjp
def low(v):
    return lax.optimization_barrier(v.astype(jnp.bfloat16)).astype(jnp.float32)

@jax.custom_vjp
def low_back(v):
    return v

def low_keep(v):
    return (low(v), None)

def low_pass(kept, grad):
    return (grad,)

def back_keep(v):
    return (v, None)

def back_low(kept, grad):
    return (low(grad),)
low.defvjp(low_keep, low_pass)
low_back.defvjp(back_keep, back_low)
norm_eps = 1e-06
rope_base = 1000000.0

def matmul(left_rows, right_matrix):
    return jnp.dot(left_rows, right_matrix, precision=lax.Precision.HIGHEST, preferred_element_type=jnp.float32)

def rms_apply(stream, norm_gain):
    mean_square = lax.optimization_barrier(jnp.mean(stream * stream, axis=-1, keepdims=True))
    return stream * lax.rsqrt(mean_square + norm_eps) * norm_gain

def rope_tables(seg_vec):
    index_all = jnp.arange(seg_vec.shape[0], dtype=jnp.int32)
    starts = jnp.concatenate([jnp.ones((1,), jnp.bool_), seg_vec[1:] != seg_vec[:-1]])
    first_idx = lax.cummax(jnp.where(starts, index_all, 0).astype(jnp.int32), axis=0)
    positions = (index_all - first_idx).astype(jnp.float32)
    half_dim = HEAD // 2
    freqs = rope_base ** (-(jnp.arange(half_dim, dtype=jnp.float32) * 2.0 / HEAD))
    angles = positions[:, None] * freqs[None, :]
    return (jnp.cos(angles)[:, None, :], jnp.sin(angles)[:, None, :])

def rotate(values, cosine, sine_vals):
    half_dim = values.shape[-1] // 2
    first_half = values[..., :half_dim]
    second_half = values[..., half_dim:]
    return jnp.concatenate([first_half * cosine - second_half * sine_vals, second_half * cosine + first_half * sine_vals], axis=-1)

def attend(qkv_seq, seg_vec):
    length = qkv_seq.shape[0]
    kv_width = KV * HEAD
    cosine, sine_vals = rope_tables(seg_vec)
    queries = qkv_seq[:, :D].reshape(length, HEADS, HEAD)
    keys_all = qkv_seq[:, D:D + kv_width].reshape(length, KV, HEAD)
    values_all = qkv_seq[:, D + kv_width:].reshape(length, KV, HEAD)
    queries = low(rotate(queries, cosine, sine_vals)).reshape(length, KV, HEADS // KV, HEAD)
    keys_all = low(rotate(keys_all, cosine, sine_vals))
    score_scale = 1.0 / math.sqrt(HEAD)
    scores = jnp.einsum('qkgd,skd->kgqs', queries, keys_all, precision=lax.Precision.HIGHEST) * score_scale
    scores = low_back(scores)
    index_all = jnp.arange(length, dtype=jnp.int32)
    allowed = (seg_vec[:, None] == seg_vec[None, :]) & (index_all[:, None] >= index_all[None, :])
    scores = jnp.where(allowed[None, None], scores, -1e+30)
    probs = low(jax.nn.softmax(scores, axis=-1))
    output = jnp.einsum('kgqs,skd->qkgd', probs, values_all, precision=lax.Precision.HIGHEST)
    return output.reshape(length, D)

def attend_pair(pair_in):
    return attend(pair_in[0], pair_in[1])

def layer_forward(stream, seg_rows, gain_attn, w_qkv, b_qkv, w_out, gain_mlp, w_gate_up, w_down):
    normed_a = low(rms_apply(stream, gain_attn))
    qkv_all = low_back(low(matmul(normed_a, w_qkv) + b_qkv))
    attended = lax.map(jax.checkpoint(attend_pair), (qkv_all.reshape(-1, SEQ_LEN, QKV), seg_rows))
    attended = low_back(low(attended.reshape(-1, D)))
    stream_mid = stream + low_back(matmul(attended, w_out))
    normed_m = low(rms_apply(stream_mid, gain_mlp))
    gate_up = low_back(matmul(normed_m, w_gate_up.reshape(D, 2 * FF)))
    act_vals = low(jax.nn.silu(gate_up[:, :FF]) * gate_up[:, FF:])
    return stream_mid + low_back(matmul(act_vals, w_down))

def reference(hidden, segments, attn_gain, qkv_weight, qkv_bias, out_weight, mlp_gain, gate_up_weight, down_weight, cotangent):
    seg_rows = segments.reshape(-1, SEQ_LEN).astype(jnp.int32)

    def forward(stream, gains_attn, w_qkv, b_qkv, w_out, gains_mlp, w_gate_up, w_down):
        for layer_no in range(LAYERS):
            stream = jax.checkpoint(layer_forward)(stream, seg_rows, gains_attn[layer_no], w_qkv[layer_no], b_qkv[layer_no], w_out[layer_no], gains_mlp[layer_no], w_gate_up[layer_no], w_down[layer_no])
        return stream
    floats = tuple((array_in.astype(jnp.float32) for array_in in (hidden, attn_gain, qkv_weight, qkv_bias, out_weight, mlp_gain, gate_up_weight, down_weight)))
    outcome, pullback = jax.vjp(forward, *floats)
    grads = pullback(cotangent.astype(jnp.float32))
    return (outcome.astype(jnp.bfloat16), grads[0], grads[1], grads[2], grads[3], grads[4], grads[5], grads[6], grads[7])
```

```python
import math

import jax
import jax.numpy as jnp
from jax import lax
from jax.sharding import PartitionSpec as P

D = 896
HEADS = 14
KV = 2
HEAD = 64
LAYERS = 2
GROUP = HEADS // KV

norm_eps = 1e-06
rope_base = 1000000.0
GRID = ("row", "col")
EVERY = ("dp", "row", "col")


def dot(spec, left, right):
    return jnp.einsum(spec, left, right, preferred_element_type=jnp.float32)


def gather_grid(shard):
    rows = lax.axis_size("row")
    whole = lax.all_gather(shard, GRID, axis=0, tiled=True)
    return whole.reshape(rows, -1, shard.shape[1])


def scatter_grid(blocks):
    flat = blocks.reshape(-1, blocks.shape[-1])
    part = lax.psum_scatter(flat, GRID, scatter_dimension=0, tiled=True)
    return lax.psum(part, "dp")


def per_row(matrix):
    rows = lax.axis_size("row")
    return jnp.broadcast_to(matrix[None], (rows,) + matrix.shape)


def norm_forward(stream, gain):
    inverse = lax.rsqrt(jnp.mean(stream * stream, axis=1, keepdims=True) + norm_eps)
    return ((stream * inverse * gain).astype(jnp.bfloat16), inverse)


def norm_backward(stream, inverse, gain, grad_normed):
    gain_part = jnp.sum(grad_normed * (stream * inverse), axis=0)
    weighted = grad_normed * gain
    inner = jnp.mean(weighted * stream, axis=1, keepdims=True)
    return (weighted * inverse - stream * (inverse * inverse * inverse * inner), gain_part)


def rope_tables(seg_vec):
    index_all = jnp.arange(seg_vec.shape[0], dtype=jnp.int32)
    starts = jnp.concatenate([jnp.ones((1,), jnp.bool_), seg_vec[1:] != seg_vec[:-1]])
    first_idx = lax.cummax(jnp.where(starts, index_all, 0), axis=0)
    positions = (index_all - first_idx).astype(jnp.float32)
    half_dim = HEAD // 2
    freqs = rope_base ** (-(jnp.arange(half_dim, dtype=jnp.float32) * 2.0 / HEAD))
    angles = positions[:, None] * freqs[None, :]
    return (jnp.cos(angles)[:, None, :], jnp.sin(angles)[:, None, :])


def rotate(values, cosine, sine_vals):
    half_dim = values.shape[-1] // 2
    first_half = values[..., :half_dim]
    second_half = values[..., half_dim:]
    return jnp.concatenate(
        [
            first_half * cosine - second_half * sine_vals,
            second_half * cosine + first_half * sine_vals,
        ],
        axis=-1,
    )


def split_heads(qkv, cosine, sine_vals):
    length = qkv.shape[0]
    turned = HEADS + KV
    heads = qkv.reshape(length, turned + KV, HEAD)
    rotated = rotate(heads[:, :turned].astype(jnp.float32), cosine, sine_vals).astype(jnp.bfloat16)
    rotated = jnp.transpose(rotated, (1, 0, 2))
    queries = rotated[:HEADS].reshape(KV, GROUP * length, HEAD)
    return (queries, rotated[HEADS:], jnp.transpose(heads[:, turned:], (1, 0, 2)))


def masked_scores(queries, keys, allowed):
    length = keys.shape[1]
    scores = dot("kqd,ksd->kqs", queries, keys) * (1.0 / math.sqrt(HEAD))
    scores = scores.reshape(KV, GROUP, length, length)
    return jnp.where(allowed[None, None], scores, -1e30)


def attend_forward(heads, allowed):
    queries, keys, values = heads
    length = keys.shape[1]
    scores = masked_scores(queries, keys, allowed)
    row_max = jnp.max(scores, axis=-1, keepdims=True)
    exp_scores = jnp.exp(scores - row_max)
    exp_total = jnp.sum(exp_scores, axis=-1, keepdims=True)
    probs = (exp_scores / exp_total).astype(jnp.bfloat16)
    output = dot("kqs,ksd->kqd", probs.reshape(KV, -1, length), values).astype(jnp.bfloat16)
    output = jnp.transpose(output.reshape(HEADS, length, HEAD), (1, 0, 2))
    return (output.reshape(length, D), row_max + jnp.log(exp_total))


def attend_backward(heads, allowed, log_norm, grad_attn, cosine, sine_vals):
    queries, keys, values = heads
    length = keys.shape[1]
    scale = 1.0 / math.sqrt(HEAD)
    grads = jnp.transpose(grad_attn.reshape(length, HEADS, HEAD), (1, 0, 2))
    grads = grads.reshape(KV, GROUP * length, HEAD)
    probs = jnp.exp(masked_scores(queries, keys, allowed) - log_norm)
    grad_probs = dot("kqd,ksd->kqs", grads, values).reshape(probs.shape)
    inner = jnp.sum(probs * grad_probs, axis=-1, keepdims=True)
    grad_scores = (probs * (grad_probs - inner)).astype(jnp.bfloat16)
    grad_scores = grad_scores.reshape(KV, GROUP * length, length)
    probs = probs.astype(jnp.bfloat16).reshape(KV, GROUP * length, length)
    grad_values = dot("kqs,kqd->ksd", probs, grads)
    grad_keys = dot("kqs,kqd->ksd", grad_scores, queries) * scale
    grad_queries = dot("kqs,ksd->kqd", grad_scores, keys) * scale
    turned = jnp.concatenate([grad_queries.reshape(HEADS, length, HEAD), grad_keys], axis=0)
    turned = rotate(jnp.transpose(turned, (1, 0, 2)), cosine, -sine_vals)
    joined = jnp.concatenate([turned, jnp.transpose(grad_values, (1, 0, 2))], axis=1)
    return joined.reshape(length, -1).astype(jnp.bfloat16)


def silu_product(gate_part, up_part):
    return jax.nn.silu(gate_part) * up_part


def on_device(
    hidden,
    segments,
    attn_gain,
    qkv_weight,
    qkv_bias,
    out_weight,
    mlp_gain,
    gate_up_weight,
    down_weight,
    cotangent,
):
    rows, cols = lax.axis_size("row"), lax.axis_size("col")
    width_dev = qkv_weight.shape[1]
    qkv_dev = qkv_weight.shape[2]
    out_dev = out_weight.shape[1]
    ff_dev = down_weight.shape[1]
    weights = []
    for n in range(LAYERS):
        attn_shard = jnp.concatenate([qkv_weight[n], out_weight[n].T], axis=1)
        weights.append(
            (
                gather_grid(attn_shard),
                gather_grid(gate_up_weight[n].reshape(width_dev, 2 * ff_dev)),
                gather_grid(down_weight[n].T),
            )
        )
    gains = lax.all_gather(jnp.concatenate([attn_gain, mlp_gain]), "col", axis=1, tiled=True)
    gains = gains.astype(jnp.float32)
    biases = lax.all_gather(qkv_bias, "row", axis=1, tiled=True).astype(jnp.float32)
    route = []
    for target in range(rows * cols):
        route.append(((target % rows) * cols + target // rows, target))
    seg_vec = lax.ppermute(segments.reshape(-1), GRID, route)
    both = lax.all_to_all(
        jnp.stack([hidden, cotangent]), "col", split_axis=1, concat_axis=2, tiled=True
    )
    length = both.shape[1]
    cosine, sine_vals = rope_tables(seg_vec)
    index_all = jnp.arange(length, dtype=jnp.int32)
    allowed = (seg_vec[:, None] == seg_vec[None, :]) & (index_all[:, None] >= index_all[None, :])
    stream = both[0].astype(jnp.float32)
    saved = []
    for n in range(LAYERS):
        w_attn, w_gu, w_down = weights[n]
        w_qkv = jnp.transpose(w_attn[:, :, :qkv_dev], (1, 0, 2)).reshape(D, -1)
        w_out = jnp.transpose(w_attn[:, :, qkv_dev:], (1, 0, 2)).reshape(D, -1)
        normed_a, inverse_a = norm_forward(stream, gains[n])
        qkv = (dot("td,df->tf", normed_a, w_qkv) + biases[n]).astype(jnp.bfloat16)
        heads = split_heads(qkv, cosine, sine_vals)
        attended, log_norm = attend_forward(heads, allowed)
        stream_mid = stream + dot("th,dh->td", attended, w_out)
        normed_m, inverse_m = norm_forward(stream_mid, gains[LAYERS + n])
        gate_up = dot("rtd,rdf->rtf", per_row(normed_m), w_gu)
        act = silu_product(gate_up[..., :ff_dev], gate_up[..., ff_dev:]).astype(jnp.bfloat16)
        stream_next = stream_mid + jnp.sum(dot("rtf,rdf->rtd", act, w_down), axis=0)
        saved.append(
            (stream, inverse_a, normed_a, heads, log_norm, attended)
            + (stream_mid, inverse_m, normed_m, gate_up, act, w_qkv, w_out)
        )
        stream = stream_next
    result = stream.astype(jnp.bfloat16)
    grad_stream = both[1].astype(jnp.float32)
    weight_grads = [None] * LAYERS
    small = [None] * (3 * LAYERS)
    for n in reversed(range(LAYERS)):
        _, w_gu, w_down = weights[n]
        stream_in, inverse_a, normed_a, heads, log_norm, attended = saved[n][:6]
        stream_mid, inverse_m, normed_m, gate_up, act, w_qkv, w_out = saved[n][6:]
        grad_down = per_row(grad_stream.astype(jnp.bfloat16))
        grad_act = dot("rtd,rdf->rtf", grad_down, w_down)
        down_term = dot("rtd,rtf->rdf", grad_down, act).astype(jnp.bfloat16)
        down_part = scatter_grid(down_term)
        _, silu_back = jax.vjp(silu_product, gate_up[..., :ff_dev], gate_up[..., ff_dev:])
        grad_gu = jnp.concatenate(silu_back(grad_act), axis=2).astype(jnp.bfloat16)
        gu_term = dot("rtd,rtf->rdf", per_row(normed_m), grad_gu).astype(jnp.bfloat16)
        gu_part = scatter_grid(gu_term)
        grad_normed_m = jnp.sum(dot("rtf,rdf->rtd", grad_gu, w_gu), axis=0)
        grad_norm_m, gain_m = norm_backward(
            stream_mid, inverse_m, gains[LAYERS + n], grad_normed_m
        )
        grad_mid = grad_stream + grad_norm_m
        grad_out = grad_mid.astype(jnp.bfloat16)
        grad_attn = dot("td,dh->th", grad_out, w_out).astype(jnp.bfloat16)
        out_term = dot("td,th->dh", grad_out, attended).astype(jnp.bfloat16)
        grad_qkv = attend_backward(heads, allowed, log_norm, grad_attn, cosine, sine_vals)
        qkv_term = dot("td,tf->df", normed_a, grad_qkv).astype(jnp.bfloat16)
        attn_term = jnp.concatenate(
            [
                jnp.transpose(qkv_term.reshape(D, rows, qkv_dev), (1, 0, 2)),
                jnp.transpose(out_term.reshape(D, rows, out_dev), (1, 0, 2)),
            ],
            axis=2,
        )
        attn_part = scatter_grid(attn_term)
        grad_normed_a = dot("tf,df->td", grad_qkv, w_qkv)
        grad_norm_a, gain_a = norm_backward(stream_in, inverse_a, gains[n], grad_normed_a)
        grad_stream = grad_mid + grad_norm_a
        weight_grads[n] = (attn_part, gu_part, down_part)
        small[n] = gain_a
        small[LAYERS + n] = gain_m
        small[2 * LAYERS + n] = jnp.sum(grad_qkv, axis=0, dtype=jnp.float32)
    outcome = lax.all_to_all(result, "col", split_axis=1, concat_axis=0, tiled=True)
    grad_hidden = lax.all_to_all(grad_stream, "col", split_axis=1, concat_axis=0, tiled=True)
    total = lax.psum(jnp.concatenate(small), EVERY)
    gain_all = total[: 2 * LAYERS * D].reshape(2 * LAYERS, D)
    bias_all = total[2 * LAYERS * D :].reshape(LAYERS, -1)
    gain_dev = lax.dynamic_slice_in_dim(
        gain_all, lax.axis_index("col") * width_dev, width_dev, axis=1
    )
    bias_dev = lax.dynamic_slice_in_dim(bias_all, lax.axis_index("row") * qkv_dev, qkv_dev, axis=1)
    wide = [tuple(part.astype(jnp.float32) for part in parts) for parts in weight_grads]
    return (
        outcome,
        grad_hidden,
        gain_dev[:LAYERS],
        jnp.stack([parts[0][:, :qkv_dev] for parts in wide]),
        bias_dev,
        jnp.stack([parts[0][:, qkv_dev:].T for parts in wide]),
        gain_dev[LAYERS:],
        jnp.stack([parts[1].reshape(width_dev, 2, ff_dev) for parts in wide]),
        jnp.stack([parts[2].T for parts in wide]),
    )


def solution(mesh):
    in_specs = (
        P(("dp", "row"), "col"),
        P("dp", "col", "row", None),
        P(None, "col"),
        P(None, "col", "row"),
        P(None, "row"),
        P(None, "row", "col"),
        P(None, "col"),
        P(None, "col", None, "row"),
        P(None, "row", "col"),
        P(("dp", "row"), "col"),
    )
    out_specs = (
        P(("dp", "row"), "col"),
        P(("dp", "row"), "col"),
        P(None, "col"),
        P(None, "col", "row"),
        P(None, "row"),
        P(None, "row", "col"),
        P(None, "col"),
        P(None, "col", None, "row"),
        P(None, "row", "col"),
    )
    return jax.shard_map(
        on_device, mesh=mesh, in_specs=in_specs, out_specs=out_specs, check_vma=False
    )
```
